512 devices in a mesh: row: 16 (over y, x), col: 32 (over z, core).
Axes of the slice: x: 4, y: 4, z: 16, core: 2. Of those that a mesh axis runs over, the one named last changes fastest.
Arguments:
- tokens: bfloat16 [4096, 8192], P('row', 'col'), may hold values from -6 to 6
- w_in: bfloat16 [8192, 3, 8192], P('row', None, 'col'), may hold values from -0.0625 to 0.0625
- filt_in: float32 [7, 3, 8192], P(None, None, 'col'), may hold values from -2.4 to 2.4
- filt_mix: float32 [7, 8192], P(None, 'col'), may hold values from -2.4 to 2.4
Outputs:
- gated: bfloat16 [4096, 8192], P('row', 'col')
The draws below stay inside these ranges and needn't reach their ends.
All inputs are finite; a program needn't handle non-finite values.
Results may differ from the reference program's by a relative error of at most 0.0064.
Values may be sent and summed in bfloat16 or wider, within the bound.
A program may use at most 64 MiB of HBM per device.

```python
import jax
import jax.numpy as jnp

D = 8192
KERNEL = 7
TOKENS = 4096


def steps_of(rng, shape, cuts, smallest, top_value):
    level, own = 1.0, jax.random.fold_in(rng, 6)
    for axis_at, blocks in cuts:
        heights = jnp.exp(jax.random.uniform(jax.random.fold_in(own, axis_at), (blocks,), jnp.float32, smallest / len(cuts), top_value / len(cuts)))
        level = level * jnp.repeat(heights, shape[axis_at] // blocks).reshape([-1 if axis == axis_at else 1 for axis in range(len(shape))])
    return level


def bell_draw(rng, dims, scale, most, shards=(), dtype=jnp.bfloat16):
    gain = steps_of(rng, dims, shards, -0.22, 0.18) if shards else 1.0
    drawn = jax.random.normal(rng, dims, jnp.float32) * scale * gain
    return jnp.minimum(jnp.maximum(drawn, -most), most).astype(dtype)


def setup_inputs(seed: int = 0) -> dict:
    seeds = jax.random.split(jax.random.key(seed), 5)
    tokens = bell_draw(seeds[0], (TOKENS, D), 1.0, 6.0, ((0, 16), (1, 32)))
    w_in = bell_draw(seeds[1], (D, 3, D), D ** -0.5, 0.0625, ((0, 16), (2, 32)))
    filt_in = bell_draw(seeds[2], (KERNEL, 3, D), 0.4, 2.4, ((2, 32),), jnp.float32)
    filt_mix = bell_draw(seeds[3], (KERNEL, D), 0.4, 2.4, ((1, 32),), jnp.float32)
    return {"tokens": tokens, "w_in": w_in, "filt_in": filt_in, "filt_mix": filt_mix}


def taps(ext, filt, count):
    total = filt[0] * ext[6:6 + count]
    for shift_s in range(1, 7):
        total = total + filt[shift_s] * ext[6 - shift_s:6 - shift_s + count]
    return total


def reference(tokens, w_in, filt_in, filt_mix):
    flat = jnp.dot(tokens, w_in.reshape(D, 3 * D), preferred_element_type=jnp.float32)
    proj = flat.astype(jnp.bfloat16).reshape(TOKENS, 3, D).astype(jnp.float32)
    padded = jnp.pad(proj, ((6, 0), (0, 0), (0, 0)))
    conv = taps(padded, filt_in, TOKENS)
    prod = conv[:, 1] * conv[:, 2]
    padded_prod = jnp.pad(prod, ((6, 0), (0, 0)))
    mix = taps(padded_prod, filt_mix, TOKENS)
    return (conv[:, 0] * mix).astype(jnp.bfloat16)
```

```python
import jax
import jax.numpy as jnp
from jax import lax
from jax.experimental import pallas as pl
from jax.experimental.pallas import tpu as pltpu
from jax.sharding import PartitionSpec as P

MESH = pl.DeviceIdType.MESH
F32 = jnp.float32
BF16 = jnp.bfloat16

NX, NY, NZ = 4, 4, 16
TB = 256
EB = 256
WB = 512
CB = 256
HALO = 16
CHUNKS = (0, 1, 3, 2)
FAR_FIRST = (2, 1, 3)
WAVES = (
    (0, 0), (1, 0), (0, 1), (2, 0), (1, 1), (0, 2), (3, 0), (2, 1),
    (1, 2), (0, 3), (3, 1), (2, 2), (1, 3), (3, 2), (2, 3), (3, 3),
)
BEHIND = ((0, 4, -4, 8), (1, -3, 5, -7), (2, -2, 6, -6), (-1, 3, -5, 7))
GO_UP = ((1, 1, 0, 0), (1, 0, 1, 0), (1, 0, 1, 0), (0, 1, 0, 1))
GO_DOWN = ((1, 0, 1, 0), (0, 1, 0, 0), (0, 1, 0, 1), (1, 0, 1, 0))


def pick(table, m, slot):
    value = jnp.int32(table[3][slot])
    for case in (2, 1, 0):
        value = jnp.where(m == case, jnp.int32(table[case][slot]), value)
    return value


def kernel(
    tok_ref, w_ref, fin_ref, fmix_ref, out_ref,
    abuf, wbuf, part, landed, ext, prod,
    a_recv, a_sib, a_up, a_down, a_side, stage_sem,
    w_here, w_send, w_recv, p_send, p_recv, h_send, h_recv,
):
    row, col = lax.axis_index("row"), lax.axis_index("col")
    y, x = lax.div(row, 4), lax.rem(row, 4)
    z, core = lax.div(col, 2), lax.rem(col, 2)
    up = (row, lax.rem(z + 1, NZ) * 2 + core)
    down = (row, lax.rem(z + NZ - 1, NZ) * 2 + core)
    side = (row, z * 2 + 1 - core)
    y_next, y_prev = lax.rem(y + 1, NY), lax.rem(y + NY - 1, NY)
    north, south = (y_next * 4 + x, col), (y_prev * 4 + x, col)
    row_next, row_prev = (lax.rem(row + 1, 16), col), (lax.rem(row + 15, 16), col)
    across = [(y * 4 + lax.rem(x + d, NX), col) for d in (1, 2, 3)]

    barrier = pltpu.get_barrier_semaphore()
    greeted = [up, down, side, north, south, row_next, row_prev] + across
    for device in greeted:
        pl.semaphore_signal(barrier, inc=1, device_id=device, device_id_type=MESH)
    pl.semaphore_wait(barrier, len(greeted))

    def send(src, dst, send_sem, recv_sem, device):
        return pltpu.make_async_remote_copy(
            src_ref=src, dst_ref=dst, send_sem=send_sem, recv_sem=recv_sem,
            device_id=device, device_id_type=MESH,
        )

    m = lax.rem(z + NZ - x, 4)
    feeds = m == 0
    jz = lax.div(z, 4)
    home = abuf.at[jz, core, pl.ds(pl.multiple_of(x * TB, TB), TB)]
    stay = pltpu.make_async_copy(tok_ref, home, stage_sem.at[0])
    stage = send(tok_ref, home, stage_sem.at[1], a_recv.at[jz, x], (y * 4 + lax.rem(z, 4), col))

    @pl.when(feeds)
    def _():
        stay.start()

    @pl.when(jnp.logical_not(feeds))
    def _():
        stage.start()

    def w_rows(block, half):
        return wbuf.at[pl.ds(pl.multiple_of(block * WB + half * (WB // 2), WB // 2), WB // 2)]

    def own_half(half):
        return w_ref.at[pl.ds(half * (WB // 2), WB // 2)]

    w_stay = pltpu.make_async_copy(w_ref, wbuf.at[pl.ds(pl.multiple_of(y * WB, WB), WB)], w_here)
    w_sends = []
    for turn in range(2):
        for way, device in ((0, north), (1, south)):
            half = turn if way == 0 else 1 - turn
            w_sends.append(send(own_half(half), w_rows(y, half), w_send.at[way, half], w_recv.at[way, half], device))
    for copy in w_sends:
        copy.start()
    w_stay.start()
    on_north = send(w_rows(y_prev, 0), w_rows(y_prev, 0), w_send.at[2, 0], w_recv.at[2, 0], north)
    on_south = send(w_rows(y_next, 1), w_rows(y_next, 1), w_send.at[2, 1], w_recv.at[2, 1], south)

    def w_arrival(way, half, block):
        return send(w_rows(block, half), w_rows(block, half), w_send.at[way, half], w_recv.at[way, half], north)

    @pl.when(feeds)
    def _():
        stay.wait()

    drains = []
    for place, (chunk, slot) in enumerate(WAVES):
        if place == 6:
            w_arrival(0, 0, y_prev).wait_recv()
            on_north.start()
            w_arrival(1, 1, y_next).wait_recv()
            on_south.start()
        k = lax.rem(x + CHUNKS[chunk], 4)
        j = lax.div(lax.rem(z + 2 * NZ - x - pick(BEHIND, m, slot), NZ), 4)
        piece = abuf.at[j, core, pl.ds(pl.multiple_of(k * TB, TB), TB)]
        go_up, go_down = pick(GO_UP, m, slot) == 1, pick(GO_DOWN, m, slot) == 1
        on_up = send(piece, piece, a_up.at[chunk, slot], a_recv.at[j, k], up)
        on_down = send(piece, piece, a_down.at[chunk, slot], a_recv.at[j, k], down)
        on_side = send(piece, piece, a_side.at[chunk, slot], a_sib.at[j, k], side)
        if chunk == 0 and slot == 0:
            @pl.when(jnp.logical_not(feeds))
            def _():
                on_up.wait_recv()
        else:
            on_up.wait_recv()

        @pl.when(go_up)
        def _():
            on_up.start()

        @pl.when(go_down)
        def _():
            on_down.start()

        on_side.start()
        drains.append((go_up, on_up, go_down, on_down, on_side))

    w_stay.wait()
    w_arrival(0, 1, y_prev).wait_recv()
    w_arrival(1, 0, y_next).wait_recv()
    far = lax.rem(y + 2, NY)
    w_arrival(2, 0, far).wait_recv()
    w_arrival(2, 1, far).wait_recv()
    for j in range(4):
        for k in range(4):
            piece = abuf.at[j, 1 - core, pl.ds(k * TB, TB)]
            send(piece, piece, a_side.at[j, k], a_sib.at[j, k], side).wait_recv()

    def partial(k):
        rows = pl.ds(pl.multiple_of(k * TB, TB), TB)
        strip = jnp.concatenate([abuf[j, h, rows, :] for j in range(4) for h in range(2)], axis=1)
        return jnp.dot(strip, wbuf[...], preferred_element_type=F32)

    shares = []
    for i, distance in enumerate(FAR_FIRST):
        part[i] = partial(lax.rem(x + distance, NX)).astype(BF16)
        share = send(part.at[i], landed.at[i], p_send.at[i], p_recv.at[i], across[distance - 1])
        share.start()
        shares.append(share)
    ext[HALO:, :] = partial(x)
    for i in (1, 2, 0):
        shares[i].wait_recv()
    ext[HALO:, :] = ext[HALO:, :] + ((landed[1].astype(F32) + landed[2].astype(F32)) + landed[0].astype(F32))

    halo = send(ext.at[pl.ds(TB, HALO)], ext.at[pl.ds(0, HALO)], h_send, h_recv, row_next)
    halo.start()
    halo.wait()

    @pl.when(row == 0)
    def _():
        ext[:HALO, :] = jnp.zeros((HALO, 3 * CB), F32)

    def taps(group, lanes, first, count):
        at = pl.ds(group * CB + lanes, 128)
        total = fin_ref[0:1, at] * ext[first : first + count, at]
        for s in range(1, 7):
            total = total + fin_ref[s : s + 1, at] * ext[first - s : first - s + count, at]
        return total

    for lanes in range(0, CB, 128):
        at = pl.ds(lanes, 128)
        prod[:, at] = taps(1, lanes, 8, TB + 8) * taps(2, lanes, 8, TB + 8)
        mix = fmix_ref[0:1, at] * prod[8 : 8 + TB, at]
        for s in range(1, 7):
            mix = mix + fmix_ref[s : s + 1, at] * prod[8 - s : 8 - s + TB, at]
        out_ref[:, at] = (taps(0, lanes, HALO, TB) * mix).astype(BF16)

    for share in shares:
        share.wait_send()
    for copy in w_sends + [on_north, on_south]:
        copy.wait_send()

    @pl.when(jnp.logical_not(feeds))
    def _():
        stage.wait_send()

    for go_up, on_up, go_down, on_down, on_side in drains:
        pl.when(go_up)(on_up.wait_send)
        pl.when(go_down)(on_down.wait_send)
        on_side.wait_send()


def per_device(tokens, w_in, filt_in, filt_mix):
    vmem = pl.BlockSpec(memory_space=pltpu.VMEM)
    dma = pltpu.SemaphoreType.DMA
    return pl.pallas_call(
        kernel,
        out_shape=jax.ShapeDtypeStruct((TB, CB), BF16),
        in_specs=[vmem] * 4,
        out_specs=vmem,
        scratch_shapes=[
            pltpu.VMEM((4, 2, NX * TB, EB), BF16),
            pltpu.VMEM((NY * WB, 3 * CB), BF16),
            pltpu.VMEM((3, TB, 3 * CB), BF16),
            pltpu.VMEM((3, TB, 3 * CB), BF16),
            pltpu.VMEM((HALO + TB, 3 * CB), F32),
            pltpu.VMEM((TB + 8, CB), F32),
            dma((4, 4)), dma((4, 4)), dma((4, 4)), dma((4, 4)), dma((4, 4)), dma((2,)),
            dma, dma((3, 2)), dma((3, 2)), dma((3,)), dma((3,)), dma, dma,
        ],
        compiler_params=pltpu.CompilerParams(collective_id=0, has_side_effects=True),
    )(tokens, w_in.reshape(WB, 3 * CB), filt_in.reshape(7, 3 * CB), filt_mix)


def solution(mesh):
    return jax.shard_map(
        per_device,
        mesh=mesh,
        in_specs=(P("row", "col"), P("row", None, "col"), P(None, None, "col"), P(None, "col")),
        out_specs=P("row", "col"),
        check_vma=False,
    )
```

```python
import jax
import jax.numpy as jnp
from jax import lax
from jax.experimental import pallas as pl
from jax.experimental.pallas import tpu as pltpu
from jax.sharding import PartitionSpec as P

MESH = pl.DeviceIdType.MESH
F32 = jnp.float32
BF16 = jnp.bfloat16

NX, NY, NZ = 4, 4, 16
TB = 256
EB = 256
WB = 512
CB = 256
HALO = 16
FAR_FIRST = (2, 1, 3)
W_HOP = 2
CUTS = 2
PT = TB // CUTS
UP, DOWN = NZ // 2, NZ // 2 - 1


def kernel(
    tok_ref, w_ref, fin_ref, fmix_ref, out_ref,
    abuf, wbuf, part, landed, ext, prod,
    stage_sem, stage_send, stage_recv, a_send, a_recv, s_send, s_recv,
    w_here, w_send, w_recv, p_send, p_recv, h_send, h_recv,
):
    row, col = lax.axis_index("row"), lax.axis_index("col")
    y, x = lax.div(row, 4), lax.rem(row, 4)
    z, core = lax.div(col, 2), lax.rem(col, 2)
    up = (row, lax.rem(z + 1, NZ) * 2 + core)
    down = (row, lax.rem(z + NZ - 1, NZ) * 2 + core)
    side = (row, z * 2 + 1 - core)
    y_next, y_prev = lax.rem(y + 1, NY), lax.rem(y + NY - 1, NY)
    north, south = (y_next * 4 + x, col), (y_prev * 4 + x, col)
    row_next, row_prev = (lax.rem(row + 1, 16), col), (lax.rem(row + 15, 16), col)
    across = [(y * 4 + lax.rem(x + d, NX), col) for d in (1, 2, 3)]

    twin_x, twin_z = lax.rem(z, 4), lax.div(z, 4) * 4 + x
    twin = (y * 4 + twin_x, twin_z * 2 + core)
    alone = twin_x == x

    barrier = pltpu.get_barrier_semaphore()
    greeted = [up, down, side, north, south, row_next, row_prev] + across
    for device in greeted:
        pl.semaphore_signal(barrier, inc=1, device_id=device, device_id_type=MESH)

    @pl.when(jnp.logical_not(alone))
    def _():
        pl.semaphore_signal(barrier, inc=1, device_id=twin, device_id_type=MESH)

    pl.semaphore_wait(barrier, len(greeted) + 1 - alone.astype(jnp.int32))

    def send(src, dst, send_sem, recv_sem, device):
        return pltpu.make_async_remote_copy(
            src_ref=src, dst_ref=dst, send_sem=send_sem, recv_sem=recv_sem,
            device_id=device, device_id_type=MESH,
        )

    def piece(block, half, cut):
        return abuf.at[block, half, pl.ds(cut * PT, PT)]

    stay = pltpu.make_async_copy(tok_ref, abuf.at[z, core], stage_sem)
    swaps = [
        send(
            tok_ref.at[pl.ds(cut * PT, PT)], piece(twin_z, core, cut),
            stage_send.at[cut], stage_recv.at[cut], twin,
        )
        for cut in range(CUTS)
    ]

    @pl.when(alone)
    def _():
        stay.start()

    @pl.when(jnp.logical_not(alone))
    def _():
        for copy in swaps:
            copy.start()

    def w_rows(block, half):
        return wbuf.at[:, pl.ds(pl.multiple_of(block * WB + half * (WB // 2), WB // 2), WB // 2)]

    def own_half(half):
        return w_ref.at[:, pl.ds(half * (WB // 2), WB // 2)]

    w_stay = pltpu.make_async_copy(w_ref, wbuf.at[:, pl.ds(pl.multiple_of(y * WB, WB), WB)], w_here)
    w_sends = []
    for turn in range(2):
        for way, device in ((0, north), (1, south)):
            half = turn if way == 0 else 1 - turn
            w_sends.append(send(own_half(half), w_rows(y, half), w_send.at[way, half], w_recv.at[way, half], device))
    for copy in w_sends:
        copy.start()
    w_stay.start()
    on_north = send(w_rows(y_prev, 0), w_rows(y_prev, 0), w_send.at[2, 0], w_recv.at[2, 0], north)
    on_south = send(w_rows(y_next, 1), w_rows(y_next, 1), w_send.at[2, 1], w_recv.at[2, 1], south)

    def w_arrival(way, half, block):
        return send(w_rows(block, half), w_rows(block, half), w_send.at[way, half], w_recv.at[way, half], north)

    @pl.when(alone)
    def _():
        stay.wait()

    sent = []

    def pass_on(way, hop, cut):
        block = lax.rem(z + NZ - hop if way == 0 else z + hop, NZ)
        here = piece(block, core, cut)
        limit, device = (UP, up) if way == 0 else (DOWN, down)
        if hop:
            send(here, here, a_send.at[way, 0, cut], a_recv.at[way, hop - 1, cut], device).wait_recv()
        if hop < limit:
            on = send(here, here, a_send.at[way, hop, cut], a_recv.at[way, hop, cut], device)
            on.start()
            sent.append(on)
        if hop or way == 0:
            place = hop if way == 0 else UP + hop
            to_side = send(here, here, s_send.at[place, cut], s_recv.at[block, cut], side)
            to_side.start()
            sent.append(to_side)

    for hop in range(UP + 1):
        for cut in range(CUTS):
            if hop == 0:
                @pl.when(jnp.logical_not(alone))
                def _():
                    send(piece(z, core, cut), piece(z, core, cut), stage_send.at[cut], stage_recv.at[cut], twin).wait_recv()
            pass_on(0, hop, cut)
            if hop <= DOWN:
                pass_on(1, hop, cut)
        if hop == W_HOP:
            w_arrival(0, 0, y_prev).wait_recv()
            on_north.start()
            w_arrival(1, 1, y_next).wait_recv()
            on_south.start()

    w_stay.wait()
    w_arrival(0, 1, y_prev).wait_recv()
    w_arrival(1, 0, y_next).wait_recv()
    far = lax.rem(y + 2, NY)
    w_arrival(2, 0, far).wait_recv()
    w_arrival(2, 1, far).wait_recv()
    for block in range(NZ):
        for cut in range(CUTS):
            there = piece(block, 1 - core, cut)
            send(there, there, s_send.at[block, cut], s_recv.at[block, cut], side).wait_recv()

    def partial(k):
        strip = jnp.concatenate([abuf[j * 4 + k, h] for j in range(4) for h in range(2)], axis=1)
        return [jnp.dot(strip, wbuf[g], preferred_element_type=F32) for g in range(3)]

    shares = []
    for i, distance in enumerate(FAR_FIRST):
        for g, product in enumerate(partial(lax.rem(x + distance, NX))):
            part[i, :, g * CB : (g + 1) * CB] = product.astype(BF16)
        share = send(part.at[i], landed.at[i], p_send.at[i], p_recv.at[i], across[distance - 1])
        share.start()
        shares.append(share)
    for g, product in enumerate(partial(x)):
        ext[HALO:, g * CB : (g + 1) * CB] = product
    for i in (1, 2, 0):
        shares[i].wait_recv()
    ext[HALO:, :] = ext[HALO:, :] + ((landed[1].astype(F32) + landed[2].astype(F32)) + landed[0].astype(F32))

    halo = send(ext.at[pl.ds(TB, HALO)], ext.at[pl.ds(0, HALO)], h_send, h_recv, row_next)
    halo.start()
    halo.wait()

    @pl.when(row == 0)
    def _():
        ext[:HALO, :] = jnp.zeros((HALO, 3 * CB), F32)

    def taps(group, lanes, first, count):
        at = pl.ds(group * CB + lanes, 128)
        own = pl.ds(lanes, 128)
        total = fin_ref[group, 0:1, own] * ext[first : first + count, at]
        for s in range(1, 7):
            total = total + fin_ref[group, s : s + 1, own] * ext[first - s : first - s + count, at]
        return total

    for lanes in range(0, CB, 128):
        at = pl.ds(lanes, 128)
        prod[:, at] = taps(1, lanes, 8, TB + 8) * taps(2, lanes, 8, TB + 8)
        mix = fmix_ref[0:1, at] * prod[8 : 8 + TB, at]
        for s in range(1, 7):
            mix = mix + fmix_ref[s : s + 1, at] * prod[8 - s : 8 - s + TB, at]
        out_ref[:, at] = (taps(0, lanes, HALO, TB) * mix).astype(BF16)

    for share in shares:
        share.wait_send()
    for copy in w_sends + [on_north, on_south]:
        copy.wait_send()

    @pl.when(jnp.logical_not(alone))
    def _():
        for copy in swaps:
            copy.wait_send()

    for copy in sent:
        copy.wait_send()


def per_device(tokens, w_in, filt_in, filt_mix):
    vmem = pl.BlockSpec(memory_space=pltpu.VMEM)
    dma = pltpu.SemaphoreType.DMA
    return pl.pallas_call(
        kernel,
        out_shape=jax.ShapeDtypeStruct((TB, CB), BF16),
        in_specs=[vmem] * 4,
        out_specs=vmem,
        scratch_shapes=[
            pltpu.VMEM((NZ, 2, TB, EB), BF16),
            pltpu.VMEM((3, NY * WB, CB), BF16),
            pltpu.VMEM((3, TB, 3 * CB), BF16),
            pltpu.VMEM((3, TB, 3 * CB), BF16),
            pltpu.VMEM((HALO + TB, 3 * CB), F32),
            pltpu.VMEM((TB + 8, CB), F32),
            dma, dma((CUTS,)), dma((CUTS,)), dma((2, UP, CUTS)), dma((2, UP, CUTS)), dma((NZ, CUTS)), dma((NZ, CUTS)),
            dma, dma((3, 2)), dma((3, 2)), dma((3,)), dma((3,)), dma, dma,
        ],
        compiler_params=pltpu.CompilerParams(collective_id=0, has_side_effects=True),
    )(tokens, jnp.transpose(w_in, (1, 0, 2)), jnp.transpose(filt_in, (1, 0, 2)), filt_mix)


def solution(mesh):
    return jax.shard_map(
        per_device,
        mesh=mesh,
        in_specs=(P("row", "col"), P("row", None, "col"), P(None, None, "col"), P(None, "col")),
        out_specs=P("row", "col"),
        check_vma=False,
    )
```

```python
import jax
import jax.numpy as jnp
from jax import lax
from jax.experimental import pallas as pl
from jax.experimental.pallas import tpu as pltpu
from jax.sharding import PartitionSpec as P

MESH = pl.DeviceIdType.MESH
F32 = jnp.float32
BF16 = jnp.bfloat16

NX, NY, NZ = 4, 4, 16
TB = 256
EB = 256
WB = 512
CB = 256
HALO = 16
FAR_FIRST = (2, 1, 3)
W_HOP = 1
CUTS = 4
PT = TB // CUTS
UP, DOWN = NZ // 2, NZ // 2 - 1


def kernel(
    tok_ref, w_ref, fin_ref, fmix_ref, out_ref,
    abuf, wbuf, part, landed, rim_part, rim_land, ext, prod,
    stage_sem, stage_send, stage_recv, a_send, a_recv, s_send, s_recv,
    w_here, w_send, w_recv, p_send, p_recv, r_send, r_recv,
):
    row, col = lax.axis_index("row"), lax.axis_index("col")
    y, x = lax.div(row, 4), lax.rem(row, 4)
    z, core = lax.div(col, 2), lax.rem(col, 2)
    up = (row, lax.rem(z + 1, NZ) * 2 + core)
    down = (row, lax.rem(z + NZ - 1, NZ) * 2 + core)
    side = (row, z * 2 + 1 - core)
    y_next, y_prev = lax.rem(y + 1, NY), lax.rem(y + NY - 1, NY)
    north, south = (y_next * 4 + x, col), (y_prev * 4 + x, col)
    heir = (y_next * 4, col)
    first = x == 0
    across = [(y * 4 + lax.rem(x + d, NX), col) for d in (1, 2, 3)]

    twin_x, twin_z = lax.rem(z, 4), lax.div(z, 4) * 4 + x
    twin = (y * 4 + twin_x, twin_z * 2 + core)
    alone = twin_x == x

    barrier = pltpu.get_barrier_semaphore()
    greeted = [up, down, side, north, south] + across
    for device in greeted + [heir]:
        pl.semaphore_signal(barrier, inc=1, device_id=device, device_id_type=MESH)

    @pl.when(jnp.logical_not(alone))
    def _():
        pl.semaphore_signal(barrier, inc=1, device_id=twin, device_id_type=MESH)

    @pl.when(first)
    def _():
        for x_from in range(NX):
            pl.semaphore_signal(barrier, inc=1, device_id=(y_prev * 4 + x_from, col), device_id_type=MESH)

    pl.semaphore_wait(barrier, len(greeted) + 2 - alone.astype(jnp.int32) + 4 * first.astype(jnp.int32))

    def send(src, dst, send_sem, recv_sem, device):
        return pltpu.make_async_remote_copy(
            src_ref=src, dst_ref=dst, send_sem=send_sem, recv_sem=recv_sem,
            device_id=device, device_id_type=MESH,
        )

    def piece(block, half, cut):
        return abuf.at[block, half, pl.ds(cut * PT, PT)]

    stay = pltpu.make_async_copy(tok_ref, abuf.at[z, core], stage_sem)
    swaps = [
        send(
            tok_ref.at[pl.ds(cut * PT, PT)], piece(twin_z, core, cut),
            stage_send.at[cut], stage_recv.at[cut], twin,
        )
        for cut in range(CUTS)
    ]

    @pl.when(alone)
    def _():
        stay.start()

    @pl.when(jnp.logical_not(alone))
    def _():
        for copy in swaps:
            copy.start()

    def w_rows(block, half):
        return wbuf.at[:, pl.ds(pl.multiple_of(block * WB + half * (WB // 2), WB // 2), WB // 2)]

    def own_half(half):
        return w_ref.at[:, pl.ds(half * (WB // 2), WB // 2)]

    w_stay = pltpu.make_async_copy(w_ref, wbuf.at[:, pl.ds(pl.multiple_of(y * WB, WB), WB)], w_here)
    w_sends = []
    for turn in range(2):
        for way, device in ((0, north), (1, south)):
            half = turn if way == 0 else 1 - turn
            w_sends.append(send(own_half(half), w_rows(y, half), w_send.at[way, half], w_recv.at[way, half], device))
    for copy in w_sends:
        copy.start()
    w_stay.start()
    on_north = send(w_rows(y_prev, 0), w_rows(y_prev, 0), w_send.at[2, 0], w_recv.at[2, 0], north)
    on_south = send(w_rows(y_next, 1), w_rows(y_next, 1), w_send.at[2, 1], w_recv.at[2, 1], south)

    def w_arrival(way, half, block):
        return send(w_rows(block, half), w_rows(block, half), w_send.at[way, half], w_recv.at[way, half], north)

    @pl.when(alone)
    def _():
        stay.wait()

    sent = []

    def pass_on(way, hop, cut):
        block = lax.rem(z + NZ - hop if way == 0 else z + hop, NZ)
        here = piece(block, core, cut)
        limit, device = (UP, up) if way == 0 else (DOWN, down)
        if hop:
            send(here, here, a_send.at[way, 0, cut], a_recv.at[way, hop - 1, cut], device).wait_recv()
        if hop < limit:
            on = send(here, here, a_send.at[way, hop, cut], a_recv.at[way, hop, cut], device)
            on.start()
            sent.append(on)
        if hop or way == 0:
            place = hop if way == 0 else UP + hop
            to_side = send(here, here, s_send.at[place, cut], s_recv.at[block, cut], side)
            to_side.start()
            sent.append(to_side)

    for hop in range(UP + 1):
        for cut in range(CUTS):
            if hop == 0:
                @pl.when(jnp.logical_not(alone))
                def _():
                    send(piece(z, core, cut), piece(z, core, cut), stage_send.at[cut], stage_recv.at[cut], twin).wait_recv()
            pass_on(0, hop, cut)
            if hop <= DOWN:
                pass_on(1, hop, cut)
        if hop == W_HOP:
            w_arrival(0, 0, y_prev).wait_recv()
            on_north.start()
            w_arrival(1, 1, y_next).wait_recv()
            on_south.start()

    w_stay.wait()
    w_arrival(0, 1, y_prev).wait_recv()
    w_arrival(1, 0, y_next).wait_recv()
    far = lax.rem(y + 2, NY)
    w_arrival(2, 0, far).wait_recv()
    w_arrival(2, 1, far).wait_recv()
    for block in range(NZ):
        for cut in range(CUTS):
            there = piece(block, 1 - core, cut)
            send(there, there, s_send.at[block, cut], s_recv.at[block, cut], side).wait_recv()

    def product(strip):
        return [jnp.dot(strip, wbuf[g], preferred_element_type=F32) for g in range(3)]

    def partial(k):
        strip = jnp.concatenate([abuf[j * 4 + k, h] for j in range(4) for h in range(2)], axis=1)
        return product(strip)

    tails = jnp.concatenate(
        [
            jnp.concatenate([abuf[j * 4 + k, h, TB - HALO :, :] for k in range(NX)], axis=0)
            for j in range(4)
            for h in range(2)
        ],
        axis=1,
    )
    for g, rows in enumerate(product(tails)):
        for k in range(NX):
            rim_part[k, :, g * CB : (g + 1) * CB] = rows[k * HALO : (k + 1) * HALO].astype(BF16)
    rims = []
    for d in (2, 1, 3):
        x_to = lax.rem(x + d, NX)
        y_to = lax.rem(y + (x_to == 0).astype(jnp.int32), NY)
        rims.append(send(rim_part.at[lax.rem(x_to + 3, NX)], rim_land.at[d], r_send.at[d], r_recv.at[d], (y_to * 4 + x_to, col)))
    own_rim = send(rim_part.at[3], rim_land.at[0], r_send.at[0], r_recv.at[0], heir)
    for rim in rims:
        rim.start()
    pl.when(first)(own_rim.start)

    shares = []
    for i, distance in enumerate(FAR_FIRST):
        for g, block in enumerate(partial(lax.rem(x + distance, NX))):
            part[i, :, g * CB : (g + 1) * CB] = block.astype(BF16)
        share = send(part.at[i], landed.at[i], p_send.at[i], p_recv.at[i], across[distance - 1])
        share.start()
        shares.append(share)
    for g, block in enumerate(partial(x)):
        ext[HALO:, g * CB : (g + 1) * CB] = block
    for i in (1, 2, 0):
        shares[i].wait_recv()
    ext[HALO:, :] = ext[HALO:, :] + ((landed[1].astype(F32) + landed[2].astype(F32)) + landed[0].astype(F32))

    @pl.when(jnp.logical_not(first))
    def _():
        rim_land[0] = rim_part[lax.rem(x + 3, NX)]

    pl.when(first)(own_rim.wait_recv)
    for rim in rims:
        rim.wait_recv()
    ext[:HALO, :] = (rim_land[0].astype(F32) + rim_land[1].astype(F32)) + (rim_land[2].astype(F32) + rim_land[3].astype(F32))

    @pl.when(row == 0)
    def _():
        ext[:HALO, :] = jnp.zeros((HALO, 3 * CB), F32)

    def taps(group, lanes, first, count):
        at = pl.ds(group * CB + lanes, 128)
        own = pl.ds(lanes, 128)
        total = fin_ref[group, 0:1, own] * ext[first : first + count, at]
        for s in range(1, 7):
            total = total + fin_ref[group, s : s + 1, own] * ext[first - s : first - s + count, at]
        return total

    for lanes in range(0, CB, 128):
        at = pl.ds(lanes, 128)
        prod[:, at] = taps(1, lanes, 8, TB + 8) * taps(2, lanes, 8, TB + 8)
        mix = fmix_ref[0:1, at] * prod[8 : 8 + TB, at]
        for s in range(1, 7):
            mix = mix + fmix_ref[s : s + 1, at] * prod[8 - s : 8 - s + TB, at]
        out_ref[:, at] = (taps(0, lanes, HALO, TB) * mix).astype(BF16)

    for share in shares + rims:
        share.wait_send()
    pl.when(first)(own_rim.wait_send)
    for copy in w_sends + [on_north, on_south]:
        copy.wait_send()

    @pl.when(jnp.logical_not(alone))
    def _():
        for copy in swaps:
            copy.wait_send()

    for copy in sent:
        copy.wait_send()


def per_device(tokens, w_in, filt_in, filt_mix):
    vmem = pl.BlockSpec(memory_space=pltpu.VMEM)
    dma = pltpu.SemaphoreType.DMA
    return pl.pallas_call(
        kernel,
        out_shape=jax.ShapeDtypeStruct((TB, CB), BF16),
        in_specs=[vmem] * 4,
        out_specs=vmem,
        scratch_shapes=[
            pltpu.VMEM((NZ, 2, TB, EB), BF16),
            pltpu.VMEM((3, NY * WB, CB), BF16),
            pltpu.VMEM((3, TB, 3 * CB), BF16),
            pltpu.VMEM((3, TB, 3 * CB), BF16),
            pltpu.VMEM((NX, HALO, 3 * CB), BF16),
            pltpu.VMEM((NX, HALO, 3 * CB), BF16),
            pltpu.VMEM((HALO + TB, 3 * CB), F32),
            pltpu.VMEM((TB + 8, CB), F32),
            dma, dma((CUTS,)), dma((CUTS,)), dma((2, UP, CUTS)), dma((2, UP, CUTS)), dma((NZ, CUTS)), dma((NZ, CUTS)),
            dma, dma((3, 2)), dma((3, 2)), dma((3,)), dma((3,)), dma((NX,)), dma((NX,)),
        ],
        compiler_params=pltpu.CompilerParams(collective_id=0, has_side_effects=True),
    )(tokens, jnp.transpose(w_in, (1, 0, 2)), jnp.transpose(filt_in, (1, 0, 2)), filt_mix)


def solution(mesh):
    return jax.shard_map(
        per_device,
        mesh=mesh,
        in_specs=(P("row", "col"), P("row", None, "col"), P(None, None, "col"), P(None, "col")),
        out_specs=P("row", "col"),
        check_vma=False,
    )
```

```python
import jax
import jax.numpy as jnp
from jax import lax
from jax.experimental import pallas as pl
from jax.experimental.pallas import tpu as pltpu
from jax.sharding import PartitionSpec as P

MESH = pl.DeviceIdType.MESH
F32 = jnp.float32
BF16 = jnp.bfloat16

NX, NY, NZ = 4, 4, 16
TB = 256
EB = 256
WB = 512
CB = 256
HALO = 16
W_HOP = 1
CUTS = 4
PT = TB // CUTS
UP, DOWN = NZ // 2, NZ // 2 - 1


def kernel(
    tok_ref, w_ref, fin_ref, fmix_ref, out_ref,
    abuf, wbuf, part, landed, rim_part, rim_land, ext, prod,
    stage_sem, stage_send, stage_recv, a_send, a_recv, s_send, s_recv,
    w_here, w_send, w_recv, p_send, p_recv, r_send, r_recv,
):
    row, col = lax.axis_index("row"), lax.axis_index("col")
    y, x = lax.div(row, 4), lax.rem(row, 4)
    z, core = lax.div(col, 2), lax.rem(col, 2)
    up = (row, lax.rem(z + 1, NZ) * 2 + core)
    down = (row, lax.rem(z + NZ - 1, NZ) * 2 + core)
    side = (row, z * 2 + 1 - core)
    y_next, y_prev = lax.rem(y + 1, NY), lax.rem(y + NY - 1, NY)
    north, south = (y_next * 4 + x, col), (y_prev * 4 + x, col)
    heir = (y_next * 4, col)
    first = x == 0
    across = [(y * 4 + lax.rem(x + d, NX), col) for d in (1, 2, 3)]

    twin_x, twin_z = lax.rem(z, 4), lax.div(z, 4) * 4 + x
    twin = (y * 4 + twin_x, twin_z * 2 + core)
    alone = twin_x == x

    barrier = pltpu.get_barrier_semaphore()
    greeted = [up, down, side, north, south] + across
    for device in greeted + [heir]:
        pl.semaphore_signal(barrier, inc=1, device_id=device, device_id_type=MESH)

    @pl.when(jnp.logical_not(alone))
    def _():
        pl.semaphore_signal(barrier, inc=1, device_id=twin, device_id_type=MESH)

    @pl.when(first)
    def _():
        for x_from in range(NX):
            pl.semaphore_signal(barrier, inc=1, device_id=(y_prev * 4 + x_from, col), device_id_type=MESH)

    pl.semaphore_wait(barrier, len(greeted) + 2 - alone.astype(jnp.int32) + 4 * first.astype(jnp.int32))

    def send(src, dst, send_sem, recv_sem, device):
        return pltpu.make_async_remote_copy(
            src_ref=src, dst_ref=dst, send_sem=send_sem, recv_sem=recv_sem,
            device_id=device, device_id_type=MESH,
        )

    def piece(block, half, cut):
        return abuf.at[block, half, pl.ds(cut * PT, PT)]

    stay = pltpu.make_async_copy(tok_ref, abuf.at[z, core], stage_sem)
    swaps = [
        send(
            tok_ref.at[pl.ds(cut * PT, PT)], piece(twin_z, core, cut),
            stage_send.at[cut], stage_recv.at[cut], twin,
        )
        for cut in range(CUTS)
    ]

    @pl.when(alone)
    def _():
        stay.start()

    @pl.when(jnp.logical_not(alone))
    def _():
        for copy in swaps:
            copy.start()

    def w_rows(block, half):
        return wbuf.at[:, pl.ds(pl.multiple_of(block * WB + half * (WB // 2), WB // 2), WB // 2)]

    def own_half(half):
        return w_ref.at[:, pl.ds(half * (WB // 2), WB // 2)]

    w_stay = pltpu.make_async_copy(w_ref, wbuf.at[:, pl.ds(pl.multiple_of(y * WB, WB), WB)], w_here)
    w_sends = []
    for turn in range(2):
        for way, device in ((0, north), (1, south)):
            half = turn if way == 0 else 1 - turn
            w_sends.append(send(own_half(half), w_rows(y, half), w_send.at[way, half], w_recv.at[way, half], device))
    for copy in w_sends:
        copy.start()
    w_stay.start()
    on_north = send(w_rows(y_prev, 0), w_rows(y_prev, 0), w_send.at[2, 0], w_recv.at[2, 0], north)
    on_south = send(w_rows(y_next, 1), w_rows(y_next, 1), w_send.at[2, 1], w_recv.at[2, 1], south)

    def w_arrival(way, half, block):
        return send(w_rows(block, half), w_rows(block, half), w_send.at[way, half], w_recv.at[way, half], north)

    @pl.when(alone)
    def _():
        stay.wait()

    sent = []

    def pass_on(way, hop, cut):
        block = lax.rem(z + NZ - hop if way == 0 else z + hop, NZ)
        here = piece(block, core, cut)
        limit, device = (UP, up) if way == 0 else (DOWN, down)
        if hop:
            send(here, here, a_send.at[way, 0, cut], a_recv.at[way, hop - 1, cut], device).wait_recv()
        if hop < limit:
            on = send(here, here, a_send.at[way, hop, cut], a_recv.at[way, hop, cut], device)
            on.start()
            sent.append(on)

    def to_side(way, hop):
        here = abuf.at[lax.rem(z + NZ - hop if way == 0 else z + hop, NZ), core]
        place = hop if way == 0 else UP + hop
        across_chip = send(here, here, s_send.at[place], s_recv.at[lax.rem(z + NZ - hop if way == 0 else z + hop, NZ)], side)
        across_chip.start()
        sent.append(across_chip)

    def product(strip):
        return [jnp.dot(strip, wbuf[g], preferred_element_type=F32) for g in range(3)]

    shares = []

    def share_out(i, step):
        k = lax.rem(z + step, NX)
        distance = lax.rem(k + NX - x, NX)
        mine, slot = distance == 0, lax.rem(distance + 3, NX)
        for j in range(4):
            there = abuf.at[j * 4 + k, 1 - core]
            send(there, there, s_send.at[j * 4 + k], s_recv.at[j * 4 + k], side).wait_recv()
        strip = jnp.concatenate([abuf[j * 4 + k, h] for j in range(4) for h in range(2)], axis=1)
        share = send(part.at[i], landed.at[slot], p_send.at[i], p_recv.at[slot], (y * 4 + k, col))
        sums = product(strip)

        @pl.when(mine)
        def _():
            for g in range(3):
                ext[HALO:, g * CB : (g + 1) * CB] = sums[g]

        @pl.when(jnp.logical_not(mine))
        def _():
            for g in range(3):
                part[i, :, g * CB : (g + 1) * CB] = sums[g].astype(BF16)
            share.start()

        shares.append((jnp.logical_not(mine), share))

    for hop in range(UP + 1):
        for cut in range(CUTS):
            if hop == 0:
                @pl.when(jnp.logical_not(alone))
                def _():
                    send(piece(z, core, cut), piece(z, core, cut), stage_send.at[cut], stage_recv.at[cut], twin).wait_recv()
            pass_on(0, hop, cut)
            if hop <= DOWN:
                pass_on(1, hop, cut)
        to_side(0, hop)
        if 0 < hop <= DOWN:
            to_side(1, hop)
        if hop == W_HOP:
            w_arrival(0, 0, y_prev).wait_recv()
            on_north.start()
            w_arrival(1, 1, y_next).wait_recv()
            on_south.start()
        if hop == UP - 2:
            w_stay.wait()
            w_arrival(0, 1, y_prev).wait_recv()
            w_arrival(1, 0, y_next).wait_recv()
            far = lax.rem(y + 2, NY)
            w_arrival(2, 0, far).wait_recv()
            w_arrival(2, 1, far).wait_recv()
            share_out(0, 2)
        if hop == UP - 1:
            share_out(1, 1)
            share_out(2, 3)
        if hop == UP:
            share_out(3, 0)

    tails = jnp.concatenate(
        [
            jnp.concatenate([abuf[j * 4 + k, h, TB - HALO :, :] for k in range(NX)], axis=0)
            for j in range(4)
            for h in range(2)
        ],
        axis=1,
    )
    for g, rows in enumerate(product(tails)):
        for k in range(NX):
            rim_part[k, :, g * CB : (g + 1) * CB] = rows[k * HALO : (k + 1) * HALO].astype(BF16)
    rims = []
    for d in (2, 1, 3):
        x_to = lax.rem(x + d, NX)
        y_to = lax.rem(y + (x_to == 0).astype(jnp.int32), NY)
        rims.append(send(rim_part.at[lax.rem(x_to + 3, NX)], rim_land.at[d], r_send.at[d], r_recv.at[d], (y_to * 4 + x_to, col)))
    own_rim = send(rim_part.at[3], rim_land.at[0], r_send.at[0], r_recv.at[0], heir)
    for rim in rims:
        rim.start()
    pl.when(first)(own_rim.start)

    for i in range(3):
        send(landed.at[i], landed.at[i], p_send.at[i], p_recv.at[i], side).wait_recv()
    ext[HALO:, :] = ext[HALO:, :] + ((landed[1].astype(F32) + landed[2].astype(F32)) + landed[0].astype(F32))

    @pl.when(jnp.logical_not(first))
    def _():
        rim_land[0] = rim_part[lax.rem(x + 3, NX)]

    pl.when(first)(own_rim.wait_recv)
    for rim in rims:
        rim.wait_recv()
    ext[:HALO, :] = (rim_land[0].astype(F32) + rim_land[1].astype(F32)) + (rim_land[2].astype(F32) + rim_land[3].astype(F32))

    @pl.when(row == 0)
    def _():
        ext[:HALO, :] = jnp.zeros((HALO, 3 * CB), F32)

    def taps(group, lanes, first, count):
        at = pl.ds(group * CB + lanes, 128)
        own = pl.ds(lanes, 128)
        total = fin_ref[group, 0:1, own] * ext[first : first + count, at]
        for s in range(1, 7):
            total = total + fin_ref[group, s : s + 1, own] * ext[first - s : first - s + count, at]
        return total

    for lanes in range(0, CB, 128):
        at = pl.ds(lanes, 128)
        prod[:, at] = taps(1, lanes, 8, TB + 8) * taps(2, lanes, 8, TB + 8)
        mix = fmix_ref[0:1, at] * prod[8 : 8 + TB, at]
        for s in range(1, 7):
            mix = mix + fmix_ref[s : s + 1, at] * prod[8 - s : 8 - s + TB, at]
        out_ref[:, at] = (taps(0, lanes, HALO, TB) * mix).astype(BF16)

    for sends, share in shares:
        pl.when(sends)(share.wait_send)
    for rim in rims:
        rim.wait_send()
    pl.when(first)(own_rim.wait_send)
    for copy in w_sends + [on_north, on_south]:
        copy.wait_send()

    @pl.when(jnp.logical_not(alone))
    def _():
        for copy in swaps:
            copy.wait_send()

    for copy in sent:
        copy.wait_send()


def per_device(tokens, w_in, filt_in, filt_mix):
    vmem = pl.BlockSpec(memory_space=pltpu.VMEM)
    dma = pltpu.SemaphoreType.DMA
    return pl.pallas_call(
        kernel,
        out_shape=jax.ShapeDtypeStruct((TB, CB), BF16),
        in_specs=[vmem] * 4,
        out_specs=vmem,
        scratch_shapes=[
            pltpu.VMEM((NZ, 2, TB, EB), BF16),
            pltpu.VMEM((3, NY * WB, CB), BF16),
            pltpu.VMEM((NX, TB, 3 * CB), BF16),
            pltpu.VMEM((NX, TB, 3 * CB), BF16),
            pltpu.VMEM((NX, HALO, 3 * CB), BF16),
            pltpu.VMEM((NX, HALO, 3 * CB), BF16),
            pltpu.VMEM((HALO + TB, 3 * CB), F32),
            pltpu.VMEM((TB + 8, CB), F32),
            dma, dma((CUTS,)), dma((CUTS,)), dma((2, UP, CUTS)), dma((2, UP, CUTS)), dma((NZ,)), dma((NZ,)),
            dma, dma((3, 2)), dma((3, 2)), dma((NX,)), dma((NX,)), dma((NX,)), dma((NX,)),
        ],
        compiler_params=pltpu.CompilerParams(collective_id=0, has_side_effects=True),
    )(tokens, jnp.transpose(w_in, (1, 0, 2)), jnp.transpose(filt_in, (1, 0, 2)), filt_mix)


def solution(mesh):
    return jax.shard_map(
        per_device,
        mesh=mesh,
        in_specs=(P("row", "col"), P("row", None, "col"), P(None, None, "col"), P(None, "col")),
        out_specs=P("row", "col"),
        check_vma=False,
    )
```

```python
import jax
import jax.numpy as jnp
from jax import lax
from jax.experimental import pallas as pl
from jax.experimental.pallas import tpu as pltpu
from jax.sharding import PartitionSpec as P

MESH = pl.DeviceIdType.MESH
F32 = jnp.float32
BF16 = jnp.bfloat16

NX, NY, NZ = 4, 4, 16
TB = 256
EB = 256
WB = 512
CB = 256
HALO = 16
FAR_FIRST = (2, 1, 3)
W_HOP = 1
CUTS = 4
PT = TB // CUTS
UP, DOWN = NZ // 2, NZ // 2 - 1


def kernel(
    tok_ref, w_ref, fin_ref, fmix_ref, out_ref,
    abuf, wbuf, part, landed, rim_part, rim_land, ext, prod,
    stage_sem, stage_send, stage_recv, a_send, a_recv, s_send, s_recv,
    w_here, w_send, w_recv, p_send, p_recv, r_send, r_recv,
):
    row, col = lax.axis_index("row"), lax.axis_index("col")
    y, x = lax.div(row, 4), lax.rem(row, 4)
    z, core = lax.div(col, 2), lax.rem(col, 2)
    up = (row, lax.rem(z + 1, NZ) * 2 + core)
    down = (row, lax.rem(z + NZ - 1, NZ) * 2 + core)
    side = (row, z * 2 + 1 - core)
    y_next, y_prev = lax.rem(y + 1, NY), lax.rem(y + NY - 1, NY)
    north, south = (y_next * 4 + x, col), (y_prev * 4 + x, col)
    heir = (y_next * 4, col)
    first = x == 0
    across = [(y * 4 + lax.rem(x + d, NX), col) for d in (1, 2, 3)]

    twin_x, twin_z = lax.rem(z, 4), lax.div(z, 4) * 4 + x
    twin = (y * 4 + twin_x, twin_z * 2 + core)
    alone = twin_x == x

    barrier = pltpu.get_barrier_semaphore()
    greeted = [up, down, side, north, south] + across
    for device in greeted + [heir]:
        pl.semaphore_signal(barrier, inc=1, device_id=device, device_id_type=MESH)

    @pl.when(jnp.logical_not(alone))
    def _():
        pl.semaphore_signal(barrier, inc=1, device_id=twin, device_id_type=MESH)

    @pl.when(first)
    def _():
        for x_from in range(NX):
            pl.semaphore_signal(barrier, inc=1, device_id=(y_prev * 4 + x_from, col), device_id_type=MESH)

    pl.semaphore_wait(barrier, len(greeted) + 2 - alone.astype(jnp.int32) + 4 * first.astype(jnp.int32))

    def send(src, dst, send_sem, recv_sem, device):
        return pltpu.make_async_remote_copy(
            src_ref=src, dst_ref=dst, send_sem=send_sem, recv_sem=recv_sem,
            device_id=device, device_id_type=MESH,
        )

    def piece(block, half, cut):
        return abuf.at[block, half, pl.ds(cut * PT, PT)]

    stay = pltpu.make_async_copy(tok_ref, abuf.at[z, core], stage_sem)
    swaps = [
        send(
            tok_ref.at[pl.ds(cut * PT, PT)], piece(twin_z, core, cut),
            stage_send.at[cut], stage_recv.at[cut], twin,
        )
        for cut in range(CUTS)
    ]

    @pl.when(alone)
    def _():
        stay.start()

    @pl.when(jnp.logical_not(alone))
    def _():
        for copy in swaps:
            copy.start()

    def w_rows(block, half):
        return wbuf.at[:, pl.ds(pl.multiple_of(block * WB + half * (WB // 2), WB // 2), WB // 2)]

    def own_half(half):
        return w_ref.at[:, pl.ds(half * (WB // 2), WB // 2)]

    w_stay = pltpu.make_async_copy(w_ref, wbuf.at[:, pl.ds(pl.multiple_of(y * WB, WB), WB)], w_here)
    w_sends = []
    for turn in range(2):
        for way, device in ((0, north), (1, south)):
            half = turn if way == 0 else 1 - turn
            w_sends.append(send(own_half(half), w_rows(y, half), w_send.at[way, half], w_recv.at[way, half], device))
    for copy in w_sends:
        copy.start()
    w_stay.start()
    on_north = send(w_rows(y_prev, 0), w_rows(y_prev, 0), w_send.at[2, 0], w_recv.at[2, 0], north)
    on_south = send(w_rows(y_next, 1), w_rows(y_next, 1), w_send.at[2, 1], w_recv.at[2, 1], south)

    def w_arrival(way, half, block):
        return send(w_rows(block, half), w_rows(block, half), w_send.at[way, half], w_recv.at[way, half], north)

    @pl.when(alone)
    def _():
        stay.wait()

    sent = []

    def pass_on(way, hop, cut):
        block = lax.rem(z + NZ - hop if way == 0 else z + hop, NZ)
        here = piece(block, core, cut)
        limit, device = (UP, up) if way == 0 else (DOWN, down)
        if hop:
            send(here, here, a_send.at[way, 0, cut], a_recv.at[way, hop - 1, cut], device).wait_recv()
        if hop < limit:
            on = send(here, here, a_send.at[way, hop, cut], a_recv.at[way, hop, cut], device)
            on.start()
            sent.append(on)

    def to_side(way, hop):
        here = abuf.at[lax.rem(z + NZ - hop if way == 0 else z + hop, NZ), core]
        place = hop if way == 0 else UP + hop
        across_chip = send(here, here, s_send.at[place], s_recv.at[lax.rem(z + NZ - hop if way == 0 else z + hop, NZ)], side)
        across_chip.start()
        sent.append(across_chip)

    for hop in range(UP + 1):
        for cut in range(CUTS):
            if hop == 0:
                @pl.when(jnp.logical_not(alone))
                def _():
                    send(piece(z, core, cut), piece(z, core, cut), stage_send.at[cut], stage_recv.at[cut], twin).wait_recv()
            pass_on(0, hop, cut)
            if hop <= DOWN:
                pass_on(1, hop, cut)
        to_side(0, hop)
        if 0 < hop <= DOWN:
            to_side(1, hop)
        if hop == W_HOP:
            w_arrival(0, 0, y_prev).wait_recv()
            on_north.start()
            w_arrival(1, 1, y_next).wait_recv()
            on_south.start()

    w_stay.wait()
    w_arrival(0, 1, y_prev).wait_recv()
    w_arrival(1, 0, y_next).wait_recv()
    far = lax.rem(y + 2, NY)
    w_arrival(2, 0, far).wait_recv()
    w_arrival(2, 1, far).wait_recv()
    for block in range(NZ):
        there = abuf.at[block, 1 - core]
        send(there, there, s_send.at[block], s_recv.at[block], side).wait_recv()

    def product(strip):
        return [jnp.dot(strip, wbuf[g], preferred_element_type=F32) for g in range(3)]

    def partial(k):
        strip = jnp.concatenate([abuf[j * 4 + k, h] for j in range(4) for h in range(2)], axis=1)
        return product(strip)

    tails = jnp.concatenate(
        [
            jnp.concatenate([abuf[j * 4 + k, h, TB - HALO :, :] for k in range(NX)], axis=0)
            for j in range(4)
            for h in range(2)
        ],
        axis=1,
    )
    for g, rows in enumerate(product(tails)):
        for k in range(NX):
            rim_part[k, :, g * CB : (g + 1) * CB] = rows[k * HALO : (k + 1) * HALO].astype(BF16)
    rims = []
    for d in (2, 1, 3):
        x_to = lax.rem(x + d, NX)
        y_to = lax.rem(y + (x_to == 0).astype(jnp.int32), NY)
        rims.append(send(rim_part.at[lax.rem(x_to + 3, NX)], rim_land.at[d], r_send.at[d], r_recv.at[d], (y_to * 4 + x_to, col)))
    own_rim = send(rim_part.at[3], rim_land.at[0], r_send.at[0], r_recv.at[0], heir)
    for rim in rims:
        rim.start()
    pl.when(first)(own_rim.start)

    shares = []
    for i, distance in enumerate(FAR_FIRST):
        for g, block in enumerate(partial(lax.rem(x + distance, NX))):
            part[i, :, g * CB : (g + 1) * CB] = block.astype(BF16)
        share = send(part.at[i], landed.at[i], p_send.at[i], p_recv.at[i], across[distance - 1])
        share.start()
        shares.append(share)
    for g, block in enumerate(partial(x)):
        ext[HALO:, g * CB : (g + 1) * CB] = block
    for i in (1, 2, 0):
        shares[i].wait_recv()
    ext[HALO:, :] = ext[HALO:, :] + ((landed[1].astype(F32) + landed[2].astype(F32)) + landed[0].astype(F32))

    @pl.when(jnp.logical_not(first))
    def _():
        rim_land[0] = rim_part[lax.rem(x + 3, NX)]

    pl.when(first)(own_rim.wait_recv)
    for rim in rims:
        rim.wait_recv()
    ext[:HALO, :] = (rim_land[0].astype(F32) + rim_land[1].astype(F32)) + (rim_land[2].astype(F32) + rim_land[3].astype(F32))

    @pl.when(row == 0)
    def _():
        ext[:HALO, :] = jnp.zeros((HALO, 3 * CB), F32)

    def taps(group, lanes, first, count):
        at = pl.ds(group * CB + lanes, 128)
        own = pl.ds(lanes, 128)
        total = fin_ref[group, 0:1, own] * ext[first : first + count, at]
        for s in range(1, 7):
            total = total + fin_ref[group, s : s + 1, own] * ext[first - s : first - s + count, at]
        return total

    for lanes in range(0, CB, 128):
        at = pl.ds(lanes, 128)
        prod[:, at] = taps(1, lanes, 8, TB + 8) * taps(2, lanes, 8, TB + 8)
        mix = fmix_ref[0:1, at] * prod[8 : 8 + TB, at]
        for s in range(1, 7):
            mix = mix + fmix_ref[s : s + 1, at] * prod[8 - s : 8 - s + TB, at]
        out_ref[:, at] = (taps(0, lanes, HALO, TB) * mix).astype(BF16)

    for share in shares + rims:
        share.wait_send()
    pl.when(first)(own_rim.wait_send)
    for copy in w_sends + [on_north, on_south]:
        copy.wait_send()

    @pl.when(jnp.logical_not(alone))
    def _():
        for copy in swaps:
            copy.wait_send()

    for copy in sent:
        copy.wait_send()


def per_device(tokens, w_in, filt_in, filt_mix):
    vmem = pl.BlockSpec(memory_space=pltpu.VMEM)
    dma = pltpu.SemaphoreType.DMA
    return pl.pallas_call(
        kernel,
        out_shape=jax.ShapeDtypeStruct((TB, CB), BF16),
        in_specs=[vmem] * 4,
        out_specs=vmem,
        scratch_shapes=[
            pltpu.VMEM((NZ, 2, TB, EB), BF16),
            pltpu.VMEM((3, NY * WB, CB), BF16),
            pltpu.VMEM((3, TB, 3 * CB), BF16),
            pltpu.VMEM((3, TB, 3 * CB), BF16),
            pltpu.VMEM((NX, HALO, 3 * CB), BF16),
            pltpu.VMEM((NX, HALO, 3 * CB), BF16),
            pltpu.VMEM((HALO + TB, 3 * CB), F32),
            pltpu.VMEM((TB + 8, CB), F32),
            dma, dma((CUTS,)), dma((CUTS,)), dma((2, UP, CUTS)), dma((2, UP, CUTS)), dma((NZ,)), dma((NZ,)),
            dma, dma((3, 2)), dma((3, 2)), dma((3,)), dma((3,)), dma((NX,)), dma((NX,)),
        ],
        compiler_params=pltpu.CompilerParams(collective_id=0, has_side_effects=True),
    )(tokens, jnp.transpose(w_in, (1, 0, 2)), jnp.transpose(filt_in, (1, 0, 2)), filt_mix)


def solution(mesh):
    return jax.shard_map(
        per_device,
        mesh=mesh,
        in_specs=(P("row", "col"), P("row", None, "col"), P(None, None, "col"), P(None, "col")),
        out_specs=P("row", "col"),
        check_vma=False,
    )
```
